32 devices in a mesh: row: 4 (over x, core), col: 8 (over z, y).
Axes of the slice: x: 2, y: 2, z: 4, core: 2. Of those that a mesh axis runs over, the one named last changes fastest.
Arguments:
- near: float32 [8, 16, 3, 3, 256, 256], P('row', 'col'), may hold values from -0.01 to 3.7
- interp: float32 [8, 16, 160, 160], P('row', 'col'), may hold values from -0.5 to 0.5
- red_count: int32 [8, 16], P('row', 'col'), may hold values from 96 to 160
- owner_flip: int32 [4, 8, 2], P('row', 'col'), may hold values from 0 to 1, as said below
Outputs:
- parents: float32 [4, 8, 640, 640], P('row', 'col')
The draws below stay inside these ranges and needn't reach their ends.
Inputs may be any that keep to these rules, and one draw needn't show every extreme that they name: owner_flip[i, j, :] is the same on the four devices of each aligned 2 x 2 group, rows 2 i and 2 i + 1, columns 2 j and 2 j + 1.
All inputs are finite; a program needn't handle non-finite values.
Results may differ from the reference program's by a relative error of at most 0.0001.
Values sent between devices are 32-bit elements; how exact they have to be, the bound alone decides.
A program may use at most 128 MiB of HBM per device.

```python
import math
import jax
import jax.numpy as jnp
from jax import lax

PTS = 256
SLOTS = 160
LOW = 96
BR = 8
BC = 16
N_ROW = 4
N_COL = 8


FORWARD = ((0, 1), (1, -1), (1, 0), (1, 1))


def draw_near(key, part):
    offsets = jax.random.uniform(jax.random.fold_in(key, 101), (BR, BC, 2, PTS), jnp.float32)
    coefficient = jnp.exp(jax.random.uniform(jax.random.fold_in(key, 102), (BR, BC, PTS), jnp.float32, math.log(0.2), math.log(0.6)))
    diag_values = jax.random.uniform(jax.random.fold_in(key, 103), (BR, BC, PTS), jnp.float32, 1.0, 2.0)
    row_places = jnp.arange(BR, dtype=jnp.int32).astype(jnp.float32)
    col_places = jnp.arange(BC, dtype=jnp.int32).astype(jnp.float32)
    pos_x = row_places[:, None, None] + offsets[:, :, 0, :]
    pos_y = col_places[None, :, None] + offsets[:, :, 1, :]
    pad_x = jnp.pad(pos_x, ((1, 1), (1, 1), (0, 0)))
    pad_y = jnp.pad(pos_y, ((1, 1), (1, 1), (0, 0)))
    pad_coef = jnp.pad(coefficient, ((1, 1), (1, 1), (0, 0)))
    identity = jnp.eye(PTS, dtype=jnp.float32)
    store = jnp.zeros((BR, BC, 3, 3, PTS, PTS), jnp.float32)
    for row_step in (-1, 0, 1):
        for col_step in (-1, 0, 1):
            other_x = pad_x[1 + row_step:1 + row_step + BR, 1 + col_step:1 + col_step + BC]
            other_y = pad_y[1 + row_step:1 + row_step + BR, 1 + col_step:1 + col_step + BC]
            other_coef = pad_coef[1 + row_step:1 + row_step + BR, 1 + col_step:1 + col_step + BC]
            delta_x = pos_x[:, :, :, None] - other_x[:, :, None, :]
            delta_y = pos_y[:, :, :, None] - other_y[:, :, None, :]
            distance = jnp.sqrt(delta_x * delta_x + delta_y * delta_y)
            block = coefficient[:, :, :, None] * other_coef[:, :, None, :] * jnp.exp(-distance / 0.5)
            if row_step == 0 and col_step == 0:
                block = block + identity * diag_values[:, :, :, None]
            store = store.at[:, :, row_step + 1, col_step + 1].set(block)
    valid = jnp.pad(jnp.ones((BR, BC), jnp.float32), ((1, 1), (1, 1)))
    for number, (row_step, col_step) in enumerate(FORWARD):
        rough = jax.random.uniform(jax.random.fold_in(key, 110 + number), (BR, BC, PTS, PTS), jnp.float32, -0.01, 0.01)
        valid_here = valid[1 + row_step:1 + row_step + BR, 1 + col_step:1 + col_step + BC]
        rough = rough * valid_here[:, :, None, None]
        store = store.at[:, :, 1 + row_step, 1 + col_step].add(rough)
        padded_rough = jnp.pad(rough, ((1, 1), (1, 1), (0, 0), (0, 0)))
        behind = padded_rough[1 - row_step:1 - row_step + BR, 1 - col_step:1 - col_step + BC]
        store = store.at[:, :, 1 - row_step, 1 - col_step].add(jnp.swapaxes(behind, 2, 3))
    rough_centre = jax.random.uniform(jax.random.fold_in(key, 120), (BR, BC, PTS, PTS), jnp.float32, -0.01, 0.01)
    store = store.at[:, :, 1, 1].add(0.5 * (rough_centre + jnp.swapaxes(rough_centre, 2, 3)))
    return store


def draw_red_count(key, part):
    base_counts = jax.random.randint(jax.random.fold_in(key, 201), (BR * BC,), PTS - SLOTS, SLOTS + 1)
    shuffled = jax.random.permutation(jax.random.fold_in(key, 202), BR * BC)
    base_counts = base_counts.at[shuffled[0]].set(PTS - SLOTS)
    base_counts = base_counts.at[shuffled[1]].set(SLOTS)
    return base_counts.reshape(BR, BC).astype(jnp.int32)


def draw_owner_flip(key, part):
    groups = jax.random.randint(jax.random.fold_in(key, 301), (BR // 4 * (BC // 4), 2), 0, 2)
    groups = groups.at[0].set(jnp.array([0, 1], dtype=jnp.int32))
    groups = groups.at[1].set(jnp.array([1, 0], dtype=jnp.int32))
    groups = groups.reshape(BR // 4, BC // 4, 2)
    spread = jnp.repeat(jnp.repeat(groups, 2, axis=0), 2, axis=1)
    return spread.astype(jnp.int32)


def block_scale(key, shape, pieces, low, high):
    def one(axis_at, shards_of):
        draws = jax.random.uniform(jax.random.fold_in(jax.random.fold_in(key, 6), axis_at), (shards_of,), jnp.float32, low / len(pieces), high / len(pieces))
        return jnp.repeat(jnp.exp(draws), shape[axis_at] // shards_of).reshape((-1,) + (1,) * (len(shape) - axis_at - 1))

    loudness = one(*pieces[0])
    for cut in pieces[1:]:
        loudness = loudness * one(*cut)
    return loudness


def normal_values(stream_key, dims, width, most, pieces=(), kind=jnp.bfloat16):
    values = width * jax.random.normal(stream_key, dims, jnp.float32)
    if pieces:
        values = values * block_scale(stream_key, dims, pieces, -0.22, 0.18)
    return jnp.clip(values, -most, most).astype(kind)


def setup_inputs(seed: int = 0) -> dict:
    key_list = jax.random.split(jax.random.key(seed), 5)
    near = draw_near(jax.random.fold_in(key_list[4], 71), 0)
    interp = normal_values(key_list[1], (BR, BC, SLOTS, SLOTS), 0.08, 0.5, ((0, 4), (1, 8)), jnp.float32)
    red_count = draw_red_count(jax.random.fold_in(key_list[4], 71), 0)
    owner_flip = draw_owner_flip(jax.random.fold_in(key_list[4], 71), 0)
    return {"near": near, "interp": interp, "red_count": red_count, "owner_flip": owner_flip}


COLOURS = ((0, 0), (0, 1), (1, 0), (1, 1))
STEPS = (-1, 0, 1)
PRECISE = lax.Precision.HIGHEST

def reference(near, interp, red_count, owner_flip):
    store = jnp.pad(near, ((1, 1), (1, 1), (0, 0), (0, 0), (0, 0), (0, 0)))
    slot_index = jnp.arange(SLOTS, dtype=jnp.int32)
    point_index = jnp.arange(PTS, dtype=jnp.int32)
    identity = jnp.eye(SLOTS, dtype=jnp.float32)
    for colour, (home_row, home_col) in enumerate(COLOURS):
        blocks = store[1 + home_row:1 + home_row + BR:2, 1 + home_col:1 + home_col + BC:2]
        red_here = red_count[home_row::2, home_col::2]
        mask_red = (slot_index[None, None, :] < red_here[:, :, None]).astype(jnp.float32)
        mask_skel = (slot_index[None, None, :] + LOW >= red_here[:, :, None]).astype(jnp.float32)
        interp_masked = interp[home_row::2, home_col::2] * mask_red[:, :, :, None] * mask_skel[:, :, None, :]
        reduced = blocks[:, :, :, :, :SLOTS, :] - jnp.einsum('ijrs,ijabst->ijabrt', interp_masked, blocks[:, :, :, :, LOW:, :], precision=PRECISE)
        active_rows = []
        for row_step in STEPS:
            line_list = []
            for col_step in STEPS:
                if row_step == 0 and col_step == 0:
                    active_here = point_index[None, None, :] >= red_here[:, :, None]
                else:
                    active_here = jnp.ones((N_ROW, N_COL, PTS), dtype=bool)
                line_list.append(active_here.astype(jnp.float32))
            active_rows.append(jnp.stack(line_list, axis=2))
        active = jnp.stack(active_rows, axis=2)
        inner_rows = reduced * mask_red[:, :, None, None, :, None] * active[:, :, :, :, None, :]
        centre = reduced[:, :, 1, 1]
        red_block = centre[:, :, :, :SLOTS] - jnp.einsum('ijrt,ijqt->ijrq', centre[:, :, :, LOW:], interp_masked, precision=PRECISE)
        both_masks = mask_red[:, :, :, None] * mask_red[:, :, None, :]
        padded = jnp.where(both_masks > 0, red_block, identity)
        lower_factor = jnp.linalg.cholesky(padded)
        stacked = inner_rows.transpose(0, 1, 4, 2, 3, 5).reshape(N_ROW, N_COL, SLOTS, 9 * PTS)
        solved = jax.scipy.linalg.solve_triangular(lower_factor, stacked, lower=True)
        panels = solved.reshape(N_ROW, N_COL, SLOTS, 3, 3, PTS)
        for row_first in STEPS:
            for col_first in STEPS:
                row_low = max(row_first - 1, -1)
                row_high = min(row_first + 1, 1)
                col_low = max(col_first - 1, -1)
                col_high = min(col_first + 1, 1)
                single = panels[:, :, :, row_first + 1, col_first + 1, :]
                paired = panels[:, :, :, row_low + 1:row_high + 2, col_low + 1:col_high + 2, :]
                update = jnp.einsum('ijrc,ijrabd->ijabcd', single, paired, precision=PRECISE)
                target_row = 1 + home_row + row_first
                target_col = 1 + home_col + col_first
                store = store.at[target_row:target_row + BR:2, target_col:target_col + BC:2, row_low - row_first + 1:row_high - row_first + 2, col_low - col_first + 1:col_high - col_first + 2].add(-update)
    inner_store = store[1:1 + BR, 1:1 + BC]
    mask_child = (slot_index[None, None, :] + LOW >= red_count[:, :, None]).astype(jnp.float32)
    row_blocks = []
    for first_row, first_col in COLOURS:
        line_list = []
        for second_row, second_col in COLOURS:
            piece_block = inner_store[first_row::2, first_col::2, second_row - first_row + 1, second_col - first_col + 1, LOW:, LOW:]
            piece_block = piece_block * mask_child[first_row::2, first_col::2][:, :, :, None] * mask_child[second_row::2, second_col::2][:, :, None, :]
            line_list.append(piece_block)
        row_blocks.append(jnp.concatenate(line_list, axis=3))
    parent = jnp.concatenate(row_blocks, axis=2)
    device_rows = jnp.arange(N_ROW, dtype=jnp.int32)
    device_cols = jnp.arange(N_COL, dtype=jnp.int32)
    partner_rows = device_rows + 1 - 2 * (device_rows % 2)
    partner_cols = device_cols + 1 - 2 * (device_cols % 2)
    source_rows = jnp.where(owner_flip[:, :, 0] == 1, partner_rows[:, None], device_rows[:, None])
    source_cols = jnp.where(owner_flip[:, :, 1] == 1, partner_cols[None, :], device_cols[None, :])
    return parent[source_rows, source_cols]
```

```python
import functools

import jax
import jax.numpy as jnp
from jax import lax
from jax.experimental import pallas as pl
from jax.experimental.pallas import tpu as pltpu
from jax.sharding import PartitionSpec as P

FULL = (-1, 1, -1, 1)
EXACT = lax.Precision.HIGHEST
GROUP = 8
BLOCK = 32


def split(value):
    high = value.astype(jnp.bfloat16)
    low = (value - high.astype(jnp.float32)).astype(jnp.bfloat16)
    return high, low


def dot(left, right):
    return jnp.dot(left, right, preferred_element_type=jnp.float32)


def product(left, right):
    left_high, left_low = left
    right_high, right_low = right
    return dot(left_high, right_high) + (dot(left_high, right_low) + dot(left_low, right_high))


def left_stack(panel):
    high, low = split(panel.T)
    return high, low


def panel_at(rect, row, col):
    return (row - rect[0]) * (rect[3] - rect[2] + 1) + col - rect[2]


def apply_source(acc, source, rect, target):
    row, col = target
    row_low, row_high = max(row - 1, rect[0]), min(row + 1, rect[1])
    col_low, col_high = max(col - 1, rect[2]), min(col + 1, rect[3])
    width = col_high - col_low + 1
    left = left_stack(source[panel_at(rect, row, col)])

    def body(i, carry):
        row_two = row_low + i // width
        col_two = col_low + i % width
        right = split(source[panel_at(rect, row_two, col_two)])
        at = (row_two - row + 1) * 3 + col_two - col + 1
        acc[at] = acc[at] - product(left, right)
        return carry

    lax.fori_loop(0, (row_high - row_low + 1) * width, body, 0)


def diagonal_inverse(block):
    size = block.shape[0]
    rows = lax.broadcasted_iota(jnp.int32, (size, size), 0)
    cols = lax.broadcasted_iota(jnp.int32, (size, size), 1)
    eye = (rows == cols).astype(jnp.float32)
    wide = jnp.concatenate([block, eye, jnp.zeros((size, 128 - 2 * size), jnp.float32)], axis=1)
    row_ids = lax.broadcasted_iota(jnp.int32, (size, 128), 0)
    scale = jnp.ones((size, 128), jnp.float32)
    for start in range(0, size, GROUP):
        columns = [
            jnp.broadcast_to(wide[:, start + q : start + q + 1], (size, 128)) for q in range(GROUP)
        ]
        for q in range(GROUP):
            at = start + q
            pivot = columns[q][at : at + 1, :]
            inverse = 1.0 / pivot
            below = jnp.where(row_ids > at, columns[q], 0.0)
            scale = jnp.where(row_ids == at, lax.rsqrt(pivot), scale)
            wide = wide - below * (wide[at : at + 1, :] * inverse)
            for p in range(q + 1, GROUP):
                columns[p] = columns[p] - below * (columns[p][at : at + 1, :] * inverse)
    return (wide * scale)[:, size : 2 * size]


def factor_inverse(matrix):
    size = matrix.shape[0]
    rows = lax.broadcasted_iota(jnp.int32, (size, size), 0)
    cols = lax.broadcasted_iota(jnp.int32, (size, size), 1)
    rest = matrix
    right = (rows == cols).astype(jnp.float32)
    done = []
    for start in range(0, size, BLOCK):
        inverse = diagonal_inverse(rest[:BLOCK, :BLOCK])
        top_right = jnp.dot(inverse, right[:BLOCK], precision=EXACT)
        done.append(top_right)
        if start + BLOCK < size:
            top = jnp.dot(inverse, rest[:BLOCK, BLOCK:], precision=EXACT)
            top_t = top.T
            rest = rest[BLOCK:, BLOCK:] - jnp.dot(top_t, top, precision=EXACT)
            right = right[BLOCK:] - jnp.dot(top_t, top_right, precision=EXACT)
    return jnp.concatenate(done, axis=0)


def eliminate_kernel(home, sources, rects_out, keep, *refs):
    n_src, n_out = len(sources), len(rects_out)
    counts, near, interp = refs[:3]
    src = refs[3 : 3 + n_src]
    outs = refs[3 + n_src : 3 + n_src + n_out]
    kept = refs[3 + n_src + n_out] if keep else None
    acc = refs[-1]
    slots = interp.shape[-1]
    points = near.shape[-1]
    low = points - slots
    if n_src:
        for k in range(9):
            acc[k] = near[k]
        for ref, (rect, target) in zip(src, sources):
            apply_source(acc, ref, rect, target)
        store = acc
    else:
        store = near
    if keep:
        for i in range(4):
            a, e = i // 2 - home[0], i % 2 - home[1]
            kept[i] = store[(a + 1) * 3 + e + 1]
    red = counts[home[0], home[1]]
    row_ids = lax.broadcasted_iota(jnp.int32, (slots, slots), 0)
    col_ids = lax.broadcasted_iota(jnp.int32, (slots, slots), 1)
    masked = jnp.where((row_ids < red) & (col_ids + low >= red), interp[...], 0.0)
    centre = store[4]
    reduced = centre[:slots] - jnp.dot(masked, centre[low:], precision=EXACT)
    block = reduced[:, :slots] - lax.dot_general(
        reduced[:, low:], masked, (((1,), (1,)), ((), ())), precision=EXACT
    )
    block = jnp.where(
        (row_ids < red) & (col_ids < red), block, (row_ids == col_ids).astype(jnp.float32)
    )
    block = 0.5 * (block + block.T)
    inverse = split(factor_inverse(block))
    interp_pair = split(masked)
    wide_rows = lax.broadcasted_iota(jnp.int32, (slots, points), 0)
    wide_cols = lax.broadcasted_iota(jnp.int32, (slots, points), 1)
    for k in range(9):
        if k == 4:
            inner = jnp.where((wide_rows < red) & (wide_cols >= red), reduced, 0.0)
        else:
            inner = store[k, :slots] - product(interp_pair, split(store[k, low:]))
            inner = jnp.where(wide_rows < red, inner, 0.0)
        panel = product(inverse, split(inner))
        row, col = k // 3 - 1, k % 3 - 1
        for ref, rect in zip(outs, rects_out):
            if rect[0] <= row <= rect[1] and rect[2] <= col <= rect[3]:
                ref[panel_at(rect, row, col)] = panel


def eliminate(home, counts, near, interp, sources, rects_out, keep):
    points, slots = near.shape[-1], interp.shape[-1]
    rects_out = [FULL] + list(rects_out)
    vmem = pl.BlockSpec(memory_space=pltpu.VMEM)
    out_shape = [
        jax.ShapeDtypeStruct(
            ((r[1] - r[0] + 1) * (r[3] - r[2] + 1), slots, points), jnp.float32
        )
        for r in rects_out
    ]
    if keep:
        out_shape.append(jax.ShapeDtypeStruct((4, points, points), jnp.float32))
    plan = [(rect, target) for _, rect, target in sources]
    return pl.pallas_call(
        functools.partial(eliminate_kernel, home, plan, rects_out, keep),
        out_shape=out_shape,
        in_specs=[pl.BlockSpec(memory_space=pltpu.SMEM)] + [vmem] * (2 + len(sources)),
        out_specs=[vmem] * len(out_shape),
        scratch_shapes=[pltpu.VMEM((9, points, points), jnp.float32)],
        compiler_params=pltpu.CompilerParams(vmem_limit_bytes=56 * 2**20),
        name="eliminate_%d%d" % home,
    )(counts, near, interp, *[array for array, _, _ in sources])


def parent_apply(acc, source, rect, shift, colour):
    boxes = [
        i
        for i in range(4)
        if rect[0] <= i // 2 - shift[0] <= rect[1] and rect[2] <= i % 2 - shift[1] <= rect[3]
    ]
    cols = sorted({i % 2 for i in boxes})
    for x in boxes:
        if x > colour:
            continue
        left = left_stack(source[panel_at(rect, x // 2 - shift[0], x % 2 - shift[1])])

        def body(i, carry, x=x, left=left):
            row = boxes[0] // 2 + i // len(cols)
            col = cols[0] + i % len(cols)
            right = split(source[panel_at(rect, row - shift[0], col - shift[1])])
            at = x * 4 + row * 2 + col
            acc[at] = acc[at] - product(left, right)
            return carry

        lax.fori_loop(0, len(boxes), body, 0)


def parent_first_kernel(plan, near, kept_one, kept_two, kept_three, *refs):
    src, out = refs[:-1], refs[-1]
    for i in range(4):
        out[i] = near[(i // 2 + 1) * 3 + i % 2 + 1]
        out[4 + i] = kept_one[i]
        out[8 + i] = kept_two[i]
        out[12 + i] = kept_three[i]
    for ref, (rect, shift, colour) in zip(src, plan):
        parent_apply(out, ref, rect, shift, colour)


def parent_last_kernel(plan, slots, counts, first, *refs):
    src, out, acc = refs[:-2], refs[-2], refs[-1]
    points = first.shape[-1]
    low = points - slots
    for i in range(16):
        acc[i] = first[i]
    for ref, (rect, shift, colour) in zip(src, plan):
        parent_apply(acc, ref, rect, shift, colour)
    row_ids = lax.broadcasted_iota(jnp.int32, (points, points), 0)
    col_ids = lax.broadcasted_iota(jnp.int32, (points, points), 1)
    for x in range(4):
        for y in range(4):
            keep = (row_ids >= counts[x // 2, x % 2]) & (col_ids >= counts[y // 2, y % 2])
            value = jnp.where(keep, acc[x * 4 + y], 0.0)
            out[x * slots : (x + 1) * slots, y * slots : (y + 1) * slots] = value[low:, low:]


def send(value, axis, by):
    peers = lax.axis_size(axis)
    pairs = [(i, i + by) for i in range(peers) if 0 <= i + by < peers]
    return lax.ppermute(value, axis, pairs)


def from_partner(value, axis):
    pairs = [(source, source ^ 1) for source in range(lax.axis_size(axis))]
    return lax.ppermute(value, axis, pairs)


def local(near, interp, red_count, owner_flip):
    points, slots = near.shape[-1], interp.shape[-1]
    boxes = near.reshape(4, 9, points, points)
    vmem = pl.BlockSpec(memory_space=pltpu.VMEM)
    smem = pl.BlockSpec(memory_space=pltpu.SMEM)

    left0, up0 = (-1, 1, -1, 0), (-1, 0, -1, 1)
    diag0 = (-1, 0, -1, 0)
    w0, l0, u0 = eliminate((0, 0), red_count, boxes[0], interp[0, 0], [], [left0, up0], False)
    l0 = send(l0, "col", -1)
    w1, r1, u1, kept1 = eliminate(
        (0, 1), red_count, boxes[1], interp[0, 1],
        [(w0, FULL, (0, 1)), (l0, left0, (0, -1))],
        [(0, 1, 0, 1), (-1, 0, -1, 1)], True,
    )
    right1, up1, diag1 = (0, 1, 0, 1), (-1, 0, -1, 1), (-1, 0, 0, 1)
    u0 = send(u0, "row", -1)
    d0 = send(l0[0:4], "row", -1)
    r1_mine = send(r1, "col", 1)
    u1 = send(u1, "row", -1)
    d1 = send(u1.reshape(2, 3, slots, points)[:, 1:].reshape(4, slots, points), "col", 1)
    w2, l2, v2, kept2 = eliminate(
        (1, 0), red_count, boxes[2], interp[1, 0],
        [
            (w0, FULL, (1, 0)), (u0, up0, (-1, 0)), (w1, FULL, (1, -1)),
            (r1_mine, right1, (1, 1)), (u1, up1, (-1, -1)), (d1, diag1, (-1, 1)),
        ],
        [(-1, 1, -1, 0), (1, 1, 0, 1)], True,
    )
    left2, down2 = (-1, 1, -1, 0), (1, 1, 0, 1)
    l2 = send(l2, "col", -1)
    v2 = send(v2, "row", 1)
    d2 = send(l2[4:5], "row", 1)
    w3, v3, r3, kept3 = eliminate(
        (1, 1), red_count, boxes[3], interp[1, 1],
        [
            (w0, FULL, (1, 1)), (l0, left0, (1, -1)), (u0, up0, (-1, 1)), (d0, diag0, (-1, -1)),
            (w1, FULL, (1, 0)), (u1, up1, (-1, 0)),
            (w2, FULL, (0, 1)), (l2, left2, (0, -1)),
        ],
        [(1, 1, -1, 0), (-1, 1, 1, 1)], True,
    )
    down3, right3 = (1, 1, -1, 0), (-1, 1, 1, 1)
    v3 = send(v3, "row", 1)
    r3 = send(r3, "col", 1)
    d3 = send(r3[2:3], "row", 1)

    plan_first = [
        (w0, FULL, (0, 0), 0), (w1, FULL, (0, 1), 1), (r1_mine, right1, (0, -1), 1),
        (w2, FULL, (1, 0), 2), (v2, down2, (-1, 0), 2), (l2, left2, (1, 2), 2),
        (d2, (1, 1, -1, -1), (-1, 2), 2), (w3, FULL, (1, 1), 3),
    ]
    first = pl.pallas_call(
        functools.partial(parent_first_kernel, [entry[1:] for entry in plan_first]),
        out_shape=jax.ShapeDtypeStruct((16, points, points), jnp.float32),
        in_specs=[vmem] * (4 + len(plan_first)),
        out_specs=vmem,
        compiler_params=pltpu.CompilerParams(vmem_limit_bytes=56 * 2**20),
        cost_estimate=pl.CostEstimate(
            flops=10 * 10**9, bytes_accessed=20 * 10**6, transcendentals=0
        ),
        name="parent_first",
    )(boxes[0], kept1, kept2, kept3, *[entry[0] for entry in plan_first])
    plan_last = [
        (v3, down3, (-1, 1), 3), (r3, right3, (1, -1), 3), (d3, (1, 1, 1, 1), (-1, -1), 3),
    ]
    parent = pl.pallas_call(
        functools.partial(parent_last_kernel, [entry[1:] for entry in plan_last], slots),
        out_shape=jax.ShapeDtypeStruct((4 * slots, 4 * slots), jnp.float32),
        in_specs=[smem] + [vmem] * (1 + len(plan_last)),
        out_specs=vmem,
        scratch_shapes=[pltpu.VMEM((16, points, points), jnp.float32)],
        compiler_params=pltpu.CompilerParams(vmem_limit_bytes=56 * 2**20),
        name="parent_last",
    )(red_count, first, *[entry[0] for entry in plan_last])
    flip = owner_flip[0, 0]
    parent = jnp.where(flip[0] == 1, from_partner(parent, "row"), parent)
    parent = jnp.where(flip[1] == 1, from_partner(parent, "col"), parent)
    return parent[None, None]


def solution(mesh):
    in_specs = (
        P("row", "col", None, None, None, None),
        P("row", "col", None, None),
        P("row", "col"),
        P("row", "col", None),
    )
    out_specs = P("row", "col", None, None)
    return jax.shard_map(local, mesh=mesh, in_specs=in_specs, out_specs=out_specs, check_vma=False)
```

```python
import functools

import jax
import jax.numpy as jnp
from jax import lax
from jax.experimental import pallas as pl
from jax.experimental.pallas import tpu as pltpu
from jax.sharding import PartitionSpec as P

FULL = (-1, 1, -1, 1)
EXACT = lax.Precision.HIGHEST
GROUP = 8
BLOCK = 32


def split(value):
    high = value.astype(jnp.bfloat16)
    low = (value - high.astype(jnp.float32)).astype(jnp.bfloat16)
    return high, low


def dot(left, right):
    return jnp.dot(left, right, preferred_element_type=jnp.float32)


def product(left, right):
    left_high, left_low = left
    right_high, right_low = right
    return dot(left_high, right_high) + (dot(left_high, right_low) + dot(left_low, right_high))


def left_stack(panel):
    high, low = split(panel.T)
    return high, low


def panel_at(rect, row, col):
    return (row - rect[0]) * (rect[3] - rect[2] + 1) + col - rect[2]


def apply_source(acc, source, rect, target):
    row, col = target
    row_low, row_high = max(row - 1, rect[0]), min(row + 1, rect[1])
    col_low, col_high = max(col - 1, rect[2]), min(col + 1, rect[3])
    width = col_high - col_low + 1
    left = left_stack(source[panel_at(rect, row, col)])

    def body(i, carry):
        row_two = row_low + i // width
        col_two = col_low + i % width
        right = split(source[panel_at(rect, row_two, col_two)])
        at = (row_two - row + 1) * 3 + col_two - col + 1
        acc[at] = acc[at] - product(left, right)
        return carry

    lax.fori_loop(0, (row_high - row_low + 1) * width, body, 0)


def diagonal_inverse(block):
    size = block.shape[0]
    rows = lax.broadcasted_iota(jnp.int32, (size, size), 0)
    cols = lax.broadcasted_iota(jnp.int32, (size, size), 1)
    eye = (rows == cols).astype(jnp.float32)
    wide = jnp.concatenate([block, eye, jnp.zeros((size, 128 - 2 * size), jnp.float32)], axis=1)
    row_ids = lax.broadcasted_iota(jnp.int32, (size, 128), 0)
    scale = jnp.ones((size, 128), jnp.float32)
    for start in range(0, size, GROUP):
        columns = [
            jnp.broadcast_to(wide[:, start + q : start + q + 1], (size, 128)) for q in range(GROUP)
        ]
        for q in range(GROUP):
            at = start + q
            pivot = columns[q][at : at + 1, :]
            inverse = 1.0 / pivot
            below = jnp.where(row_ids > at, columns[q], 0.0)
            scale = jnp.where(row_ids == at, lax.rsqrt(pivot), scale)
            wide = wide - below * (wide[at : at + 1, :] * inverse)
            for p in range(q + 1, GROUP):
                columns[p] = columns[p] - below * (columns[p][at : at + 1, :] * inverse)
    return (wide * scale)[:, size : 2 * size]


def factor_inverse(matrix):
    size = matrix.shape[0]
    rows = lax.broadcasted_iota(jnp.int32, (size, size), 0)
    cols = lax.broadcasted_iota(jnp.int32, (size, size), 1)
    rest = matrix
    right = (rows == cols).astype(jnp.float32)
    done = []
    for start in range(0, size, BLOCK):
        inverse = diagonal_inverse(rest[:BLOCK, :BLOCK])
        top_right = jnp.dot(inverse, right[:BLOCK], precision=EXACT)
        done.append(top_right)
        if start + BLOCK < size:
            top = jnp.dot(inverse, rest[:BLOCK, BLOCK:], precision=EXACT)
            top_t = top.T
            rest = rest[BLOCK:, BLOCK:] - jnp.dot(top_t, top, precision=EXACT)
            right = right[BLOCK:] - jnp.dot(top_t, top_right, precision=EXACT)
    return jnp.concatenate(done, axis=0)


def load(source, at, buffer, sem):
    view = source if at is None else source.at[at]
    copy = pltpu.make_async_copy(view, buffer, sem)
    copy.start()
    return copy


def eliminate_kernel(home, base_at, sources, rects_out, keep, n_extra, *refs):
    n_src, n_out = len(sources), len(rects_out)
    counts, base, interp_all = refs[:3]
    src = refs[3 : 3 + n_src]
    refs = refs[3 + n_src + n_extra :]
    outs = refs[:n_out]
    kept = refs[n_out] if keep else None
    store, interp, sems = refs[-3:]
    slots = interp.shape[-1]
    points = store.shape[-1]
    low = points - slots
    first = load(base, base_at, store, sems.at[0])
    second = load(interp_all, (home[0], home[1]), interp, sems.at[1])
    first.wait()
    second.wait()
    for ref, (rect, target) in zip(src, sources):
        apply_source(store, ref, rect, target)
    if keep:
        for i in range(4):
            a, e = i // 2 - home[0], i % 2 - home[1]
            kept[i] = store[(a + 1) * 3 + e + 1][low:, low:]
    red = counts[home[0], home[1]]
    row_ids = lax.broadcasted_iota(jnp.int32, (slots, slots), 0)
    col_ids = lax.broadcasted_iota(jnp.int32, (slots, slots), 1)
    masked = jnp.where((row_ids < red) & (col_ids + low >= red), interp[...], 0.0)
    centre = store[4]
    reduced = centre[:slots] - jnp.dot(masked, centre[low:], precision=EXACT)
    block = reduced[:, :slots] - lax.dot_general(
        reduced[:, low:], masked, (((1,), (1,)), ((), ())), precision=EXACT
    )
    block = jnp.where(
        (row_ids < red) & (col_ids < red), block, (row_ids == col_ids).astype(jnp.float32)
    )
    block = 0.5 * (block + block.T)
    inverse = split(factor_inverse(block))
    interp_pair = split(masked)
    wide_rows = lax.broadcasted_iota(jnp.int32, (slots, points), 0)
    wide_cols = lax.broadcasted_iota(jnp.int32, (slots, points), 1)
    for k in range(9):
        if k == 4:
            inner = jnp.where((wide_rows < red) & (wide_cols >= red), reduced, 0.0)
        else:
            inner = store[k, :slots] - product(interp_pair, split(store[k, low:]))
            inner = jnp.where(wide_rows < red, inner, 0.0)
        panel = product(inverse, split(inner))
        row, col = k // 3 - 1, k % 3 - 1
        for ref, rect in zip(outs, rects_out):
            if rect[0] <= row <= rect[1] and rect[2] <= col <= rect[3]:
                ref[panel_at(rect, row, col)] = panel


VMEM = pl.BlockSpec(memory_space=pltpu.VMEM)
SMEM = pl.BlockSpec(memory_space=pltpu.SMEM)
ANY = pl.BlockSpec(memory_space=pl.ANY)
PARAMS = pltpu.CompilerParams(vmem_limit_bytes=56 * 2**20)


def cost(products):
    return pl.CostEstimate(
        flops=products * 60 * 10**6, bytes_accessed=10**7, transcendentals=0
    )


def eliminate(home, counts, base, base_at, interp, sources, rects_out, keep, extra=()):
    points, slots = base.shape[-1], interp.shape[-1]
    rects_out = [FULL] + list(rects_out)
    out_shape = [
        jax.ShapeDtypeStruct(
            ((r[1] - r[0] + 1) * (r[3] - r[2] + 1), slots, points), jnp.float32
        )
        for r in rects_out
    ]
    if keep:
        out_shape.append(jax.ShapeDtypeStruct((4, slots, slots), jnp.float32))
    plan = [(rect, target) for _, rect, target in sources]
    return pl.pallas_call(
        functools.partial(eliminate_kernel, home, base_at, plan, rects_out, keep, len(extra)),
        out_shape=out_shape,
        in_specs=[SMEM, ANY, ANY] + [VMEM] * len(sources) + [ANY] * len(extra),
        out_specs=[VMEM] * len(out_shape),
        scratch_shapes=[
            pltpu.VMEM((9, points, points), jnp.float32),
            pltpu.VMEM((slots, slots), jnp.float32),
            pltpu.SemaphoreType.DMA((2,)),
        ],
        compiler_params=PARAMS,
        cost_estimate=cost(60),
        name="eliminate_%d%d" % home,
    )(counts, base, interp, *[array for array, _, _ in sources], *extra)


def update_kernel(jobs, n_base, n_src, *refs):
    bases, src = refs[:n_base], refs[n_base : n_base + n_src]
    outs, sems = refs[n_base + n_src : -1], refs[-1]
    copies = [
        load(bases[base], at, out, sems.at[i])
        for i, ((base, at, _), out) in enumerate(zip(jobs, outs))
    ]
    for copy, out, (_, _, work) in zip(copies, outs, jobs):
        copy.wait()
        for which, rect, target in work:
            apply_source(out, src[which], rect, target)


def update(name, bases, sources, jobs):
    points = bases[0].shape[-1]
    return pl.pallas_call(
        functools.partial(update_kernel, jobs, len(bases), len(sources)),
        out_shape=[jax.ShapeDtypeStruct((9, points, points), jnp.float32) for _ in jobs],
        in_specs=[ANY] * len(bases) + [VMEM] * len(sources),
        out_specs=[VMEM] * len(jobs),
        scratch_shapes=[pltpu.SemaphoreType.DMA((len(jobs),))],
        compiler_params=PARAMS,
        cost_estimate=cost(20),
        name=name,
    )(*bases, *sources)


def parent_apply(acc, source, rect, shift, colour):
    boxes = [
        i
        for i in range(4)
        if rect[0] <= i // 2 - shift[0] <= rect[1] and rect[2] <= i % 2 - shift[1] <= rect[3]
    ]
    cols = sorted({i % 2 for i in boxes})
    slots = acc.shape[-1]
    low = source.shape[-1] - slots
    for x in boxes:
        if x > colour:
            continue
        panel = source[panel_at(rect, x // 2 - shift[0], x % 2 - shift[1])]
        left = split(panel.T[low:])

        def body(i, carry, x=x, left=left):
            row = boxes[0] // 2 + i // len(cols)
            col = cols[0] + i % len(cols)
            right = split(source[panel_at(rect, row - shift[0], col - shift[1])][:, low:])
            at = x * 4 + row * 2 + col
            acc[at] = acc[at] - product(left, right)
            return carry

        lax.fori_loop(0, len(boxes), body, 0)


def parent_early_kernel(plan, near, kept_one, kept_two, *refs):
    src, out, buffer, sems = refs[:-3], refs[-3], refs[-2], refs[-1]
    low = buffer.shape[-1] - out.shape[-1]
    copies = [
        load(near, (0, (i // 2 + 1) * 3 + i % 2 + 1), buffer.at[i], sems.at[i]) for i in range(4)
    ]
    for i in range(4):
        copies[i].wait()
        out[i] = buffer[i][low:, low:]
        out[4 + i] = kept_one[i]
        out[8 + i] = kept_two[i]
        out[12 + i] = jnp.zeros(out.shape[1:], jnp.float32)
    for ref, (rect, shift, colour) in zip(src, plan):
        parent_apply(out, ref, rect, shift, colour)


def parent_middle_kernel(plan, early, kept_three, *refs):
    src, out = refs[:-1], refs[-1]
    for i in range(12):
        out[i] = early[i]
    for i in range(4):
        out[12 + i] = kept_three[i]
    for ref, (rect, shift, colour) in zip(src, plan):
        parent_apply(out, ref, rect, shift, colour)


def parent_last_kernel(plan, points, counts, middle, *refs):
    src, out, acc = refs[:-2], refs[-2], refs[-1]
    slots = acc.shape[-1]
    low = points - slots
    for i in range(16):
        acc[i] = middle[i]
    for ref, (rect, shift, colour) in zip(src, plan):
        parent_apply(acc, ref, rect, shift, colour)
    row_ids = lax.broadcasted_iota(jnp.int32, (slots, slots), 0) + low
    col_ids = lax.broadcasted_iota(jnp.int32, (slots, slots), 1) + low
    for x in range(4):
        for y in range(4):
            keep = (row_ids >= counts[x // 2, x % 2]) & (col_ids >= counts[y // 2, y % 2])
            out[x * slots : (x + 1) * slots, y * slots : (y + 1) * slots] = jnp.where(
                keep, acc[x * 4 + y], 0.0
            )


def send(value, axis, by):
    peers = lax.axis_size(axis)
    pairs = [(i, i + by) for i in range(peers) if 0 <= i + by < peers]
    return lax.ppermute(value, axis, pairs)


def from_partner(value, axis):
    pairs = [(source, source ^ 1) for source in range(lax.axis_size(axis))]
    return lax.ppermute(value, axis, pairs)


def local(near, interp, red_count, owner_flip):
    points, slots = near.shape[-1], interp.shape[-1]
    boxes = near.reshape(4, 9, points, points)

    left0, up0, diag0 = (-1, 1, -1, 0), (-1, 0, -1, 1), (-1, 0, -1, 0)
    right1, up1, diag1 = (0, 1, 0, 1), (-1, 0, -1, 1), (-1, 0, 0, 1)
    left2, down2 = (-1, 1, -1, 0), (1, 1, 0, 1)
    down3, right3 = (1, 1, -1, 0), (-1, 0, 1, 1)
    corner3 = (1, 1, 1, 1)

    w0, l0, u0 = eliminate(
        (0, 0), red_count, boxes, 0, interp, [], [left0, up0], False
    )
    l0 = send(l0, "col", -1)
    u0 = send(u0, "row", -1)
    acc1, acc2, acc3 = update(
        "gap_zero", [boxes], [w0],
        [(0, i, [(0, FULL, (i // 2, i % 2))]) for i in (1, 2, 3)],
    )
    w1, r1, u1, kept1 = eliminate(
        (0, 1), red_count, acc1, None, interp, [(l0, left0, (0, -1))], [right1, up1], True,
        extra=(u0,),
    )
    d0 = send(l0[0:4], "row", -1)
    r1 = send(r1, "col", 1)
    u1 = send(u1, "row", -1)
    d1 = send(u1.reshape(2, 3, slots, points)[:, 1:].reshape(4, slots, points), "col", 1)
    acc2, acc3 = update(
        "gap_one", [acc2, acc3], [u0, w1, l0],
        [
            (0, None, [(0, up0, (-1, 0)), (1, FULL, (1, -1))]),
            (1, None, [(0, up0, (-1, 1)), (1, FULL, (1, 0)), (2, left0, (1, -1))]),
        ],
    )
    w2, l2, v2, kept2 = eliminate(
        (1, 0), red_count, acc2, None, interp,
        [(r1, right1, (1, 1)), (u1, up1, (-1, -1)), (d1, diag1, (-1, 1))],
        [left2, down2], True, extra=(d0,),
    )
    l2 = send(l2, "col", -1)
    v2 = send(v2, "row", 1)
    (acc3,) = update(
        "gap_two", [acc3], [d0, u1, w2],
        [(0, None, [(0, diag0, (-1, -1)), (1, up1, (-1, 0)), (2, FULL, (0, 1))])],
    )
    plan_early = [
        (w0, FULL, (0, 0), 0), (w1, FULL, (0, 1), 1), (r1, right1, (0, -1), 1),
        (w2, FULL, (1, 0), 2),
    ]
    early = pl.pallas_call(
        functools.partial(parent_early_kernel, [entry[1:] for entry in plan_early]),
        out_shape=jax.ShapeDtypeStruct((16, slots, slots), jnp.float32),
        in_specs=[ANY] + [VMEM] * (2 + len(plan_early)),
        out_specs=VMEM,
        scratch_shapes=[
            pltpu.VMEM((4, points, points), jnp.float32), pltpu.SemaphoreType.DMA((4,)),
        ],
        compiler_params=PARAMS,
        cost_estimate=cost(30),
        name="parent_early",
    )(boxes, kept1, kept2, *[entry[0] for entry in plan_early])
    w3, v3, r3, d3, kept3 = eliminate(
        (1, 1), red_count, acc3, None, interp, [(l2, left2, (0, -1))],
        [down3, right3, corner3], True, extra=(early, v2),
    )
    v3 = send(v3, "row", 1)
    r3 = send(r3, "col", 1)
    d3 = send(send(d3, "row", 1), "col", 1)
    d2 = send(l2[4:5], "row", 1)

    plan_middle = [
        (v2, down2, (-1, 0), 2), (l2, left2, (1, 2), 2),
        (d2, (1, 1, -1, -1), (-1, 2), 2), (w3, FULL, (1, 1), 3),
    ]
    middle = pl.pallas_call(
        functools.partial(parent_middle_kernel, [entry[1:] for entry in plan_middle]),
        out_shape=jax.ShapeDtypeStruct((16, slots, slots), jnp.float32),
        in_specs=[VMEM] * (2 + len(plan_middle)),
        out_specs=VMEM,
        compiler_params=PARAMS,
        cost_estimate=cost(30),
        name="parent_middle",
    )(early, kept3, *[entry[0] for entry in plan_middle])
    plan_last = [
        (v3, down3, (-1, 1), 3), (r3, right3, (1, -1), 3), (d3, corner3, (-1, -1), 3),
    ]
    parent = pl.pallas_call(
        functools.partial(parent_last_kernel, [entry[1:] for entry in plan_last], points),
        out_shape=jax.ShapeDtypeStruct((4 * slots, 4 * slots), jnp.float32),
        in_specs=[SMEM] + [VMEM] * (1 + len(plan_last)),
        out_specs=VMEM,
        scratch_shapes=[pltpu.VMEM((16, slots, slots), jnp.float32)],
        compiler_params=PARAMS,
        cost_estimate=cost(10),
        name="parent_last",
    )(red_count, middle, *[entry[0] for entry in plan_last])
    flip = owner_flip[0, 0]
    parent = jnp.where(flip[0] == 1, from_partner(parent, "row"), parent)
    parent = jnp.where(flip[1] == 1, from_partner(parent, "col"), parent)
    return parent[None, None]


def solution(mesh):
    in_specs = (
        P("row", "col", None, None, None, None),
        P("row", "col", None, None),
        P("row", "col"),
        P("row", "col", None),
    )
    out_specs = P("row", "col", None, None)
    return jax.shard_map(local, mesh=mesh, in_specs=in_specs, out_specs=out_specs, check_vma=False)
```

```python
import functools

import jax
import jax.numpy as jnp
from jax import lax
from jax.experimental import pallas as pl
from jax.experimental.pallas import tpu as pltpu
from jax.sharding import PartitionSpec as P

FULL = (-1, 1, -1, 1)
EXACT = lax.Precision.HIGHEST
GROUP = 8
BLOCK = 32


def split(value):
    high = value.astype(jnp.bfloat16)
    low = (value - high.astype(jnp.float32)).astype(jnp.bfloat16)
    return high, low


def dot(left, right):
    return jnp.dot(left, right, preferred_element_type=jnp.float32)


def product(left, right):
    left_high, left_low = left
    right_high, right_low = right
    return dot(left_high, right_high) + (dot(left_high, right_low) + dot(left_low, right_high))


def left_stack(panel):
    high, low = split(panel.T)
    return high, low


def panel_at(rect, row, col):
    return (row - rect[0]) * (rect[3] - rect[2] + 1) + col - rect[2]


def apply_source(acc, source, rect, target):
    row, col = target
    row_low, row_high = max(row - 1, rect[0]), min(row + 1, rect[1])
    col_low, col_high = max(col - 1, rect[2]), min(col + 1, rect[3])
    width = col_high - col_low + 1
    left = left_stack(source[panel_at(rect, row, col)])

    def body(i, carry):
        row_two = row_low + i // width
        col_two = col_low + i % width
        right = split(source[panel_at(rect, row_two, col_two)])
        at = (row_two - row + 1) * 3 + col_two - col + 1
        acc[at] = acc[at] - product(left, right)
        return carry

    lax.fori_loop(0, (row_high - row_low + 1) * width, body, 0)


def diagonal_inverse(block):
    size = block.shape[0]
    rows = lax.broadcasted_iota(jnp.int32, (size, size), 0)
    cols = lax.broadcasted_iota(jnp.int32, (size, size), 1)
    eye = (rows == cols).astype(jnp.float32)
    wide = jnp.concatenate([block, eye, jnp.zeros((size, 128 - 2 * size), jnp.float32)], axis=1)
    row_ids = lax.broadcasted_iota(jnp.int32, (size, 128), 0)
    scale = jnp.ones((size, 128), jnp.float32)
    for start in range(0, size, GROUP):
        columns = [
            jnp.broadcast_to(wide[:, start + q : start + q + 1], (size, 128)) for q in range(GROUP)
        ]
        for q in range(GROUP):
            at = start + q
            pivot = columns[q][at : at + 1, :]
            inverse = 1.0 / pivot
            below = jnp.where(row_ids > at, columns[q], 0.0)
            scale = jnp.where(row_ids == at, lax.rsqrt(pivot), scale)
            wide = wide - below * (wide[at : at + 1, :] * inverse)
            for p in range(q + 1, GROUP):
                columns[p] = columns[p] - below * (columns[p][at : at + 1, :] * inverse)
    return (wide * scale)[:, size : 2 * size]


def factor_inverse(matrix):
    size = matrix.shape[0]
    rows = lax.broadcasted_iota(jnp.int32, (size, size), 0)
    cols = lax.broadcasted_iota(jnp.int32, (size, size), 1)
    rest = matrix
    right = (rows == cols).astype(jnp.float32)
    done = []
    for start in range(0, size, BLOCK):
        inverse = diagonal_inverse(rest[:BLOCK, :BLOCK])
        top_right = jnp.dot(inverse, right[:BLOCK], precision=EXACT)
        done.append(top_right)
        if start + BLOCK < size:
            top = jnp.dot(inverse, rest[:BLOCK, BLOCK:], precision=EXACT)
            top_t = top.T
            rest = rest[BLOCK:, BLOCK:] - jnp.dot(top_t, top, precision=EXACT)
            right = right[BLOCK:] - jnp.dot(top_t, top_right, precision=EXACT)
    return jnp.concatenate(done, axis=0)


def load(source, at, buffer, sem):
    view = source if at is None else source.at[at]
    copy = pltpu.make_async_copy(view, buffer, sem)
    copy.start()
    return copy


def eliminate_kernel(home, base_at, sources, rects_out, keep, n_extra, relay, *refs):
    n_src, n_out = len(sources), len(rects_out)
    counts, base, interp_all = refs[:3]
    src = refs[3 : 3 + n_src]
    refs = refs[3 + n_src + n_extra :]
    outs = refs[:n_out]
    kept = refs[n_out] if keep else None
    store, interp, sems = refs[-3:]
    slots = interp.shape[-1]
    points = store.shape[-1]
    low = points - slots
    first = load(base, base_at, store, sems.at[0])
    second = load(interp_all, (home[0], home[1]), interp, sems.at[1])
    if relay is not None:
        outs[1][outs[1].shape[0] - 1] = src[0][relay]
    first.wait()
    second.wait()
    for ref, (rect, target) in zip(src, sources):
        apply_source(store, ref, rect, target)
    if keep:
        for i in range(4):
            a, e = i // 2 - home[0], i % 2 - home[1]
            kept[i] = store[(a + 1) * 3 + e + 1][low:, low:]
    red = counts[home[0], home[1]]
    row_ids = lax.broadcasted_iota(jnp.int32, (slots, slots), 0)
    col_ids = lax.broadcasted_iota(jnp.int32, (slots, slots), 1)
    masked = jnp.where((row_ids < red) & (col_ids + low >= red), interp[...], 0.0)
    centre = store[4]
    reduced = centre[:slots] - jnp.dot(masked, centre[low:], precision=EXACT)
    block = reduced[:, :slots] - lax.dot_general(
        reduced[:, low:], masked, (((1,), (1,)), ((), ())), precision=EXACT
    )
    block = jnp.where(
        (row_ids < red) & (col_ids < red), block, (row_ids == col_ids).astype(jnp.float32)
    )
    block = 0.5 * (block + block.T)
    inverse = split(factor_inverse(block))
    interp_pair = split(masked)
    wide_rows = lax.broadcasted_iota(jnp.int32, (slots, points), 0)
    wide_cols = lax.broadcasted_iota(jnp.int32, (slots, points), 1)
    for k in range(9):
        if k == 4:
            inner = jnp.where((wide_rows < red) & (wide_cols >= red), reduced, 0.0)
        else:
            inner = store[k, :slots] - product(interp_pair, split(store[k, low:]))
            inner = jnp.where(wide_rows < red, inner, 0.0)
        panel = product(inverse, split(inner))
        row, col = k // 3 - 1, k % 3 - 1
        for ref, rect in zip(outs, rects_out):
            if rect[0] <= row <= rect[1] and rect[2] <= col <= rect[3]:
                ref[panel_at(rect, row, col)] = panel


VMEM = pl.BlockSpec(memory_space=pltpu.VMEM)
SMEM = pl.BlockSpec(memory_space=pltpu.SMEM)
ANY = pl.BlockSpec(memory_space=pl.ANY)
PARAMS = pltpu.CompilerParams(vmem_limit_bytes=56 * 2**20)


def cost(products):
    return pl.CostEstimate(
        flops=products * 60 * 10**6, bytes_accessed=10**7, transcendentals=0
    )


def eliminate(home, counts, base, base_at, interp, sources, rects_out, keep, extra=(), relay=None):
    points, slots = base.shape[-1], interp.shape[-1]
    rects_out = [FULL] + list(rects_out)
    out_shape = [
        jax.ShapeDtypeStruct(
            (
                (r[1] - r[0] + 1) * (r[3] - r[2] + 1) + (relay is not None and at == 1),
                slots,
                points,
            ),
            jnp.float32,
        )
        for at, r in enumerate(rects_out)
    ]
    if keep:
        out_shape.append(jax.ShapeDtypeStruct((4, slots, slots), jnp.float32))
    plan = [(rect, target) for _, rect, target in sources]
    return pl.pallas_call(
        functools.partial(eliminate_kernel, home, base_at, plan, rects_out, keep, len(extra), relay),
        out_shape=out_shape,
        in_specs=[SMEM, ANY, ANY] + [VMEM] * len(sources) + [ANY] * len(extra),
        out_specs=[VMEM] * len(out_shape),
        scratch_shapes=[
            pltpu.VMEM((9, points, points), jnp.float32),
            pltpu.VMEM((slots, slots), jnp.float32),
            pltpu.SemaphoreType.DMA((2,)),
        ],
        compiler_params=PARAMS,
        cost_estimate=cost(60),
        name="eliminate_%d%d" % home,
    )(counts, base, interp, *[array for array, _, _ in sources], *extra)


def update_kernel(jobs, n_base, n_src, *refs):
    bases, src = refs[:n_base], refs[n_base : n_base + n_src]
    outs, sems = refs[n_base + n_src : -1], refs[-1]
    copies = [
        load(bases[base], at, out, sems.at[i])
        for i, ((base, at, _), out) in enumerate(zip(jobs, outs))
    ]
    for copy, out, (_, _, work) in zip(copies, outs, jobs):
        copy.wait()
        for which, rect, target in work:
            apply_source(out, src[which], rect, target)


def update(name, bases, sources, jobs):
    points = bases[0].shape[-1]
    return pl.pallas_call(
        functools.partial(update_kernel, jobs, len(bases), len(sources)),
        out_shape=[jax.ShapeDtypeStruct((9, points, points), jnp.float32) for _ in jobs],
        in_specs=[ANY] * len(bases) + [VMEM] * len(sources),
        out_specs=[VMEM] * len(jobs),
        scratch_shapes=[pltpu.SemaphoreType.DMA((len(jobs),))],
        compiler_params=PARAMS,
        cost_estimate=cost(20),
        name=name,
    )(*bases, *sources)


def parent_apply(acc, source, rect, shift, colour):
    boxes = [
        i
        for i in range(4)
        if rect[0] <= i // 2 - shift[0] <= rect[1] and rect[2] <= i % 2 - shift[1] <= rect[3]
    ]
    cols = sorted({i % 2 for i in boxes})
    slots = acc.shape[-1]
    low = source.shape[-1] - slots
    for x in boxes:
        if x > colour:
            continue
        panel = source[panel_at(rect, x // 2 - shift[0], x % 2 - shift[1])]
        left = split(panel.T[low:])

        def body(i, carry, x=x, left=left):
            row = boxes[0] // 2 + i // len(cols)
            col = cols[0] + i % len(cols)
            right = split(source[panel_at(rect, row - shift[0], col - shift[1])][:, low:])
            at = x * 4 + row * 2 + col
            acc[at] = acc[at] - product(left, right)
            return carry

        lax.fori_loop(0, len(boxes), body, 0)


def parent_early_kernel(plan, near, kept_one, kept_two, *refs):
    src, out, buffer, sems = refs[:-3], refs[-3], refs[-2], refs[-1]
    low = buffer.shape[-1] - out.shape[-1]
    copies = [
        load(near, (0, (i // 2 + 1) * 3 + i % 2 + 1), buffer.at[i], sems.at[i]) for i in range(4)
    ]
    for i in range(4):
        copies[i].wait()
        out[i] = buffer[i][low:, low:]
        out[4 + i] = kept_one[i]
        out[8 + i] = kept_two[i]
        out[12 + i] = jnp.zeros(out.shape[1:], jnp.float32)
    for ref, (rect, shift, colour) in zip(src, plan):
        parent_apply(out, ref, rect, shift, colour)


def parent_middle_kernel(plan, early, kept_three, *refs):
    src, out = refs[:-1], refs[-1]
    for i in range(12):
        out[i] = early[i]
    for i in range(4):
        out[12 + i] = kept_three[i]
    for ref, (rect, shift, colour) in zip(src, plan):
        parent_apply(out, ref, rect, shift, colour)


def parent_last_kernel(plan, points, counts, middle, *refs):
    src, out, acc = refs[:-2], refs[-2], refs[-1]
    slots = acc.shape[-1]
    low = points - slots
    for i in range(16):
        acc[i] = middle[i]
    for ref, (rect, shift, colour) in zip(src, plan):
        parent_apply(acc, ref, rect, shift, colour)
    relayed = src[0][3]
    acc[5] = acc[5] - product(split(relayed.T[low:]), split(relayed[:, low:]))
    row_ids = lax.broadcasted_iota(jnp.int32, (slots, slots), 0) + low
    col_ids = lax.broadcasted_iota(jnp.int32, (slots, slots), 1) + low
    for x in range(4):
        for y in range(4):
            keep = (row_ids >= counts[x // 2, x % 2]) & (col_ids >= counts[y // 2, y % 2])
            out[x * slots : (x + 1) * slots, y * slots : (y + 1) * slots] = jnp.where(
                keep, acc[x * 4 + y], 0.0
            )


def send(value, axis, by):
    peers = lax.axis_size(axis)
    pairs = [(i, i + by) for i in range(peers) if 0 <= i + by < peers]
    return lax.ppermute(value, axis, pairs)


def from_partner(value, axis):
    pairs = [(source, source ^ 1) for source in range(lax.axis_size(axis))]
    return lax.ppermute(value, axis, pairs)


def local(near, interp, red_count, owner_flip):
    points, slots = near.shape[-1], interp.shape[-1]
    boxes = near.reshape(4, 9, points, points)

    left0, up0, diag0 = (-1, 1, -1, 0), (-1, 0, -1, 1), (-1, 0, -1, 0)
    right1, up1, diag1 = (0, 1, 0, 1), (-1, 0, -1, 1), (-1, 0, 0, 1)
    left2, down2 = (-1, 1, -1, 0), (1, 1, 0, 1)
    down3, right3 = (1, 1, -1, 1), (-1, 0, 1, 1)
    corner3 = (1, 1, 1, 1)

    w0, l0, u0 = eliminate(
        (0, 0), red_count, boxes, 0, interp, [], [left0, up0], False
    )
    l0 = send(l0, "col", -1)
    u0 = send(u0, "row", -1)
    acc1, acc2, acc3 = update(
        "gap_zero", [boxes], [w0],
        [(0, i, [(0, FULL, (i // 2, i % 2))]) for i in (1, 2, 3)],
    )
    w1, r1, u1, kept1 = eliminate(
        (0, 1), red_count, acc1, None, interp, [(l0, left0, (0, -1))], [right1, up1], True,
        extra=(u0,),
    )
    d0 = send(l0[0:4], "row", -1)
    r1 = send(r1, "col", 1)
    u1 = send(u1, "row", -1)
    d1 = send(u1.reshape(2, 3, slots, points)[:, 1:].reshape(4, slots, points), "col", 1)
    acc2, acc3 = update(
        "gap_one", [acc2, acc3], [u0, w1, l0, u1],
        [
            (0, None, [(0, up0, (-1, 0)), (1, FULL, (1, -1)), (3, up1, (-1, -1))]),
            (1, None, [
                (0, up0, (-1, 1)), (1, FULL, (1, 0)), (2, left0, (1, -1)), (3, up1, (-1, 0)),
            ]),
        ],
    )
    w2, l2, v2, kept2 = eliminate(
        (1, 0), red_count, acc2, None, interp,
        [(r1, right1, (1, 1)), (d1, diag1, (-1, 1))],
        [left2, down2], True, extra=(d0,),
    )
    l2 = send(l2, "col", -1)
    v2 = send(v2, "row", 1)
    (acc3,) = update(
        "gap_two", [acc3], [d0, w2],
        [(0, None, [(0, diag0, (-1, -1)), (1, FULL, (0, 1))])],
    )
    plan_early = [
        (w0, FULL, (0, 0), 0), (w1, FULL, (0, 1), 1), (r1, right1, (0, -1), 1),
        (w2, FULL, (1, 0), 2),
    ]
    early = pl.pallas_call(
        functools.partial(parent_early_kernel, [entry[1:] for entry in plan_early]),
        out_shape=jax.ShapeDtypeStruct((16, slots, slots), jnp.float32),
        in_specs=[ANY] + [VMEM] * (2 + len(plan_early)),
        out_specs=VMEM,
        scratch_shapes=[
            pltpu.VMEM((4, points, points), jnp.float32), pltpu.SemaphoreType.DMA((4,)),
        ],
        compiler_params=PARAMS,
        cost_estimate=cost(30),
        name="parent_early",
    )(boxes, kept1, kept2, *[entry[0] for entry in plan_early])
    w3, v3, r3, kept3 = eliminate(
        (1, 1), red_count, acc3, None, interp, [(l2, left2, (0, -1))],
        [down3, right3], True, extra=(early, v2), relay=4,
    )
    v3 = send(v3, "row", 1)
    r3 = send(r3, "col", 1)
    d3 = send(v3[2:3], "col", 1)

    plan_middle = [
        (v2, down2, (-1, 0), 2), (l2, left2, (1, 2), 2),
        (w3, FULL, (1, 1), 3),
    ]
    middle = pl.pallas_call(
        functools.partial(parent_middle_kernel, [entry[1:] for entry in plan_middle]),
        out_shape=jax.ShapeDtypeStruct((16, slots, slots), jnp.float32),
        in_specs=[VMEM] * (2 + len(plan_middle)),
        out_specs=VMEM,
        compiler_params=PARAMS,
        cost_estimate=cost(30),
        name="parent_middle",
    )(early, kept3, *[entry[0] for entry in plan_middle])
    plan_last = [
        (v3, down3, (-1, 1), 3), (r3, right3, (1, -1), 3), (d3, corner3, (-1, -1), 3),
    ]
    parent = pl.pallas_call(
        functools.partial(parent_last_kernel, [entry[1:] for entry in plan_last], points),
        out_shape=jax.ShapeDtypeStruct((4 * slots, 4 * slots), jnp.float32),
        in_specs=[SMEM] + [VMEM] * (1 + len(plan_last)),
        out_specs=VMEM,
        scratch_shapes=[pltpu.VMEM((16, slots, slots), jnp.float32)],
        compiler_params=PARAMS,
        cost_estimate=cost(10),
        name="parent_last",
    )(red_count, middle, *[entry[0] for entry in plan_last])
    flip = owner_flip[0, 0]
    parent = jnp.where(flip[0] == 1, from_partner(parent, "row"), parent)
    parent = jnp.where(flip[1] == 1, from_partner(parent, "col"), parent)
    return parent[None, None]


def solution(mesh):
    in_specs = (
        P("row", "col", None, None, None, None),
        P("row", "col", None, None),
        P("row", "col"),
        P("row", "col", None),
    )
    out_specs = P("row", "col", None, None)
    return jax.shard_map(local, mesh=mesh, in_specs=in_specs, out_specs=out_specs, check_vma=False)
```
